32 devices in a mesh: snap: 16 (over z, y, core), zone: 2 (over x).
Axes of the slice: x: 2, y: 2, z: 4, core: 2. Of those that a mesh axis runs over, the one named last changes fastest.
Arguments:
- forward: bfloat16 [2048, 2048], P('zone', 'snap'), may hold values from -40 to 40, as said below
- adjoint: bfloat16 [2048, 2048], P('zone', 'snap'), may hold values from -0.125 to 0.125
Outputs:
- rotated: float32 [2048, 2048], P('snap', 'zone')
The draws below stay inside these ranges and needn't reach their ends.
Inputs may be any that keep to these rules, and one draw needn't show every extreme that they name: `forward`: independent entries, each snapshot column with its own scale.
All inputs are finite; a program needn't handle non-finite values.
Results may differ from the reference program's by a relative error of at most 0.0003.
Values may be sent and summed in bfloat16 or wider, within the bound.
A program may use at most 64 MiB of HBM per device.

```python
import math
import jax
import jax.numpy as jnp
from jax import lax

ROUNDS = 8
HALF = 64
K = 2048
ZONES = 2048
N_SNAP = 16


def draw_forward(key, part):
    first, second = jax.random.split(key)
    base = jnp.clip(jax.random.normal(first, (ZONES, K), jnp.float32), -4.0, 4.0)
    column = jnp.exp(jax.random.uniform(second, (1, K), jnp.float32, 0.0, math.log(10.0)))
    return (base * column).astype(jnp.bfloat16)


def steps_of(own_key, dims, cuts, low, top_value):
    def one(axis_at, parts):
        heights = jax.random.uniform(jax.random.fold_in(jax.random.fold_in(own_key, 6), axis_at), (parts,), jnp.float32, low / len(cuts), top_value / len(cuts))
        return jnp.repeat(jnp.exp(heights), dims[axis_at] // parts).reshape((-1,) + (1,) * (len(dims) - axis_at - 1))

    level = one(*cuts[0])
    for cut in cuts[1:]:
        level = level * one(*cut)
    return level


def normal_values(rng, extent, deviation, bound, cuts=(), kind=jnp.bfloat16):
    result = jax.random.normal(rng, extent, jnp.float32) * deviation
    if len(cuts) > 0:
        result = steps_of(rng, extent, cuts, -0.22, 0.18) * result
    return jnp.clip(result, min=-bound, max=bound).astype(kind)


def setup_inputs(seed: int = 0) -> dict:
    keys = jax.random.split(jax.random.key(seed), 3)
    forward = draw_forward(jax.random.fold_in(keys[2], 71), 0)
    adjoint = normal_values(keys[1], (ZONES, K), ZONES ** -0.5, 0.125, ((0, 2), (1, 16)))
    return {"forward": forward, "adjoint": adjoint}


def highdot(a, b):
    return jnp.dot(a.astype(jnp.float32), b.astype(jnp.float32), precision=lax.Precision.HIGHEST, preferred_element_type=jnp.float32)

def orthogonalize(pair):
    gram = lax.dot_general(pair.astype(jnp.float32), pair.astype(jnp.float32), (((1,), (1,)), ((), ())), precision=lax.Precision.HIGHEST, preferred_element_type=jnp.float32)
    scales = jnp.sqrt(jnp.diagonal(gram) + 1e-06)
    corr = gram / (scales[:, None] * scales[None, :])
    half_rows = corr.shape[0] // 2
    block = corr[:half_rows, half_rows:]
    spread = jnp.sqrt(jnp.sum(block * block))
    coupling = 0.5 * block / jnp.maximum(spread, 1.0)
    zeros = jnp.zeros((half_rows, half_rows), jnp.float32)
    skew = jnp.concatenate([jnp.concatenate([zeros, coupling], axis=1), jnp.concatenate([-coupling.T, zeros], axis=1)], axis=0)
    ident = jnp.eye(corr.shape[0], dtype=jnp.float32)
    minus = ident - skew
    square = highdot(minus, minus)
    normal = ident + highdot(skew.T, skew)
    factor = jnp.linalg.cholesky(normal)
    middle = lax.linalg.triangular_solve(factor, square, left_side=True, lower=True)
    rotation = lax.linalg.triangular_solve(factor, middle, left_side=True, lower=True, transpose_a=True)
    return highdot(rotation, pair)

def reference(forward, adjoint):
    cross = jnp.dot(forward.astype(jnp.float32).T.astype(jnp.float32), adjoint.astype(jnp.float32), precision=lax.Precision.HIGHEST, preferred_element_type=jnp.float32)
    blocks = cross.reshape(N_SNAP, 2, HALF, K)
    top = blocks[:, 0]
    bottom = blocks[:, 1]
    for rnd in range(ROUNDS):
        pairs = jnp.concatenate([top, bottom], axis=1)
        done = jax.vmap(orthogonalize)(pairs)
        top = done[:, :HALF]
        bottom = done[:, HALF:]
        if rnd + 1 < ROUNDS:
            right = jnp.concatenate([bottom[:1], top[1:]], axis=0)
            moved = jnp.concatenate([top[:1], right[:-1]], axis=0)
            left = jnp.concatenate([bottom[1:], top[-1:]], axis=0)
            top = moved
            bottom = left
    return jnp.concatenate([top, bottom], axis=1).reshape(K, K)
```

```python
import functools

import numpy as np
import jax
import jax.numpy as jnp
from jax import lax
from jax.experimental import pallas as pl
from jax.experimental.pallas import tpu as pltpu
from jax.sharding import PartitionSpec as P

ROUNDS = 8
CHUNKS = 2
NN = (((1,), (0,)), ((), ()))
NT = (((1,), (1,)), ((), ()))


def inverse_coefficients(degree):
    cheb = np.polynomial.chebyshev.Chebyshev.basis(degree + 1).convert(kind=np.polynomial.Polynomial)
    shifted = cheb(np.polynomial.Polynomial([-1.0, 8.0]))
    residual = shifted / shifted(-1.0)
    quotient = (np.polynomial.Polynomial([1.0]) - residual) // np.polynomial.Polynomial([1.0, 1.0])
    return [float(c) for c in quotient.coef]


def split(a):
    high = a.astype(jnp.bfloat16)
    return high, (a - high.astype(jnp.float32)).astype(jnp.bfloat16)


def dot3(a, b, dims):
    (ah, al), (bh, bl) = a, b
    dot = functools.partial(lax.dot_general, dimension_numbers=dims, preferred_element_type=jnp.float32)
    return dot(ah, bh) + (dot(ah, bl) + dot(al, bh))


def rounds_kernel(n, nz, half, cw, rows_ref, out_ref, topbuf, botbuf, outtop, outbot, stats,
                  send_r, recv_t, send_l, recv_b, send_z, recv_z):
    s = lax.axis_index("snap")
    z = lax.axis_index("zone")
    coef = inverse_coefficients(6)

    barrier = pltpu.get_barrier_semaphore()

    @pl.when(s > 0)
    def _():
        pl.semaphore_signal(barrier, inc=1, device_id={"snap": s - 1}, device_id_type=pl.DeviceIdType.MESH)

    @pl.when(s < n - 1)
    def _():
        pl.semaphore_signal(barrier, inc=1, device_id={"snap": s + 1}, device_id_type=pl.DeviceIdType.MESH)

    for k in range(1, nz):
        pl.semaphore_signal(barrier, inc=1, device_id={"zone": lax.rem(z + k, nz)}, device_id_type=pl.DeviceIdType.MESH)

    for c in range(CHUNKS):
        topbuf[0, c] = rows_ref[0:half, c * cw:(c + 1) * cw]
        botbuf[0, c] = rows_ref[half:2 * half, c * cw:(c + 1) * cw]

    @pl.when((s > 0) & (s < n - 1))
    def _():
        pl.semaphore_wait(barrier, nz + 1)

    @pl.when((s == 0) | (s == n - 1))
    def _():
        pl.semaphore_wait(barrier, nz)

    def right_copy(r, c, src):
        return pltpu.make_async_remote_copy(
            src_ref=src.at[r, c], dst_ref=topbuf.at[r + 1, c], send_sem=send_r.at[r, c], recv_sem=recv_t.at[r + 1, c],
            device_id={"snap": jnp.minimum(s + 1, n - 1)}, device_id_type=pl.DeviceIdType.MESH)

    def left_copy(r, c):
        return pltpu.make_async_remote_copy(
            src_ref=outbot.at[r, c], dst_ref=botbuf.at[r + 1, c], send_sem=send_l.at[r, c], recv_sem=recv_b.at[r + 1, c],
            device_id={"snap": jnp.maximum(s - 1, 0)}, device_id_type=pl.DeviceIdType.MESH)

    def zone_copy(r, k):
        return pltpu.make_async_remote_copy(
            src_ref=stats.at[r, 0], dst_ref=stats.at[r, k], send_sem=send_z.at[r, k], recv_sem=recv_z.at[r, k],
            device_id={"zone": lax.rem(z + k, nz)}, device_id_type=pl.DeviceIdType.MESH)

    def rotate(r):
        block = None
        ones = jnp.ones((8, cw), jnp.bfloat16)
        for c in range(CHUNKS):
            top = topbuf[r, c]
            bottom = botbuf[r, c]
            part = dot3(split(top), split(bottom), NT)
            tops = jnp.sum(top * top, axis=1, keepdims=True)
            bh, bl = split(bottom * bottom)
            bots = (lax.dot_general(ones, bh, NT, preferred_element_type=jnp.float32)
                    + lax.dot_general(ones, bl, NT, preferred_element_type=jnp.float32))
            block, tsum, bsum = (part, tops, bots) if block is None else (block + part, tsum + tops, bsum + bots)
        stats[r, 0, 0:half, 0:half] = block
        stats[r, 0, 0:half, half:2 * half] = jnp.broadcast_to(tsum, (half, half))
        stats[r, 0, half:half + 8, 0:half] = bsum
        stats[r, 0, half:half + 8, half:2 * half] = bsum
        for k in range(1, nz):
            zone_copy(r, k).start()
        total = stats[r, 0]
        for k in range(1, nz):
            zone_copy(r, k).wait_recv()
            total = total + stats[r, k]
        tinv = 1.0 / jnp.sqrt(total[0:half, half:2 * half] + 1e-06)
        binv = 1.0 / jnp.sqrt(total[half:half + 1, 0:half] + 1e-06)
        corr = total[0:half, 0:half] * (tinv * binv)
        spread = jnp.sqrt(jnp.sum(corr * corr, keepdims=True))
        x = corr * (0.5 / jnp.maximum(spread, 1.0))
        xs = split(x)
        xts = split(x.T)
        ident = (lax.broadcasted_iota(jnp.int32, (half, half), 0)
                 == lax.broadcasted_iota(jnp.int32, (half, half), 1)).astype(jnp.float32)
        n1 = dot3(xs, xs, NT)
        n1s = split(n1)
        n2 = dot3(n1s, n1s, NN)
        n3 = dot3(split(n2), n1s, NN)
        upper = coef[3] * ident + coef[4] * n1 + coef[5] * n2 + coef[6] * n3
        inverse = coef[0] * ident + coef[1] * n1 + coef[2] * n2 + dot3(split(n3), split(upper), NN)
        invs = split(inverse)
        return xs, xts, invs

    def apply(r, c, parts):
        xs, xts, invs = parts
        top = topbuf[r, c]
        bottom = botbuf[r, c]
        v = top - dot3(xs, split(bottom), NN)
        w = dot3(invs, split(v), NN)
        return 2.0 * w - top, bottom + 2.0 * dot3(xts, split(w), NN)

    def step(r, carry):
        @pl.when((r > 0) & (s > 0))
        def _():
            for c in range(CHUNKS):
                right_copy(r - 1, c, outtop).wait_recv()

        @pl.when((r > 0) & (s < n - 1))
        def _():
            for c in range(CHUNKS):
                left_copy(r - 1, c).wait_recv()

        parts = rotate(r)
        for c in range(CHUNKS):
            top, bottom = apply(r, c, parts)
            outtop[r, c] = top
            outbot[r, c] = bottom

            @pl.when((s > 0) & (s < n - 1))
            def _():
                right_copy(r, c, outtop).start()

            @pl.when(s == 0)
            def _():
                right_copy(r, c, outbot).start()
                topbuf[r + 1, c] = outtop[r, c]

            @pl.when(s > 0)
            def _():
                left_copy(r, c).start()

            @pl.when(s == n - 1)
            def _():
                botbuf[r + 1, c] = outtop[r, c]
        return carry

    lax.fori_loop(0, ROUNDS - 1, step, 0)
    last = ROUNDS - 1

    @pl.when(s > 0)
    def _():
        for c in range(CHUNKS):
            right_copy(last - 1, c, outtop).wait_recv()

    @pl.when(s < n - 1)
    def _():
        for c in range(CHUNKS):
            left_copy(last - 1, c).wait_recv()

    parts = rotate(last)
    for c in range(CHUNKS):
        top, bottom = apply(last, c, parts)
        out_ref[0:half, c * cw:(c + 1) * cw] = top
        out_ref[half:2 * half, c * cw:(c + 1) * cw] = bottom

    def drain(r, carry):
        @pl.when(s < n - 1)
        def _():
            for c in range(CHUNKS):
                right_copy(r, c, outtop).wait_send()

        @pl.when(s > 0)
        def _():
            for c in range(CHUNKS):
                left_copy(r, c).wait_send()
        return carry

    lax.fori_loop(0, last, drain, 0)

    def drain_zone(r, carry):
        for k in range(1, nz):
            zone_copy(r, k).wait_send()
        return carry

    lax.fori_loop(0, ROUNDS, drain_zone, 0)


def run_rounds(rows, n, nz):
    height, width = rows.shape
    half = height // 2
    cw = width // CHUNKS
    return pl.pallas_call(
        functools.partial(rounds_kernel, n, nz, half, cw),
        out_shape=jax.ShapeDtypeStruct(rows.shape, jnp.float32),
        in_specs=[pl.BlockSpec(memory_space=pltpu.VMEM)],
        out_specs=pl.BlockSpec(memory_space=pltpu.VMEM),
        scratch_shapes=[
            pltpu.VMEM((ROUNDS, CHUNKS, half, cw), jnp.float32),
            pltpu.VMEM((ROUNDS, CHUNKS, half, cw), jnp.float32),
            pltpu.VMEM((ROUNDS - 1, CHUNKS, half, cw), jnp.float32),
            pltpu.VMEM((ROUNDS - 1, CHUNKS, half, cw), jnp.float32),
            pltpu.VMEM((ROUNDS, nz, half + 8, 2 * half), jnp.float32),
            pltpu.SemaphoreType.DMA((ROUNDS, CHUNKS)),
            pltpu.SemaphoreType.DMA((ROUNDS, CHUNKS)),
            pltpu.SemaphoreType.DMA((ROUNDS, CHUNKS)),
            pltpu.SemaphoreType.DMA((ROUNDS, CHUNKS)),
            pltpu.SemaphoreType.DMA((ROUNDS, nz)),
            pltpu.SemaphoreType.DMA((ROUNDS, nz)),
        ],
        compiler_params=pltpu.CompilerParams(
            collective_id=0, has_side_effects=True, vmem_limit_bytes=48 * 1024 * 1024),
    )(rows)


def solution(mesh):
    n, nz = mesh.shape["snap"], mesh.shape["zone"]

    def shards(forward, adjoint):
        partial_rows = lax.dot_general(
            forward,
            lax.all_gather(adjoint, "snap", axis=1, tiled=True),
            (((0,), (0,)), ((), ())),
            preferred_element_type=jnp.float32,
        )
        rows = lax.psum_scatter(partial_rows, "zone", scatter_dimension=1, tiled=True)
        return run_rounds(rows, n, nz)

    return jax.shard_map(
        shards,
        mesh=mesh,
        in_specs=(P("zone", "snap"), P("zone", "snap")),
        out_specs=P("snap", "zone"),
        check_vma=False,
    )
```

```python
import functools

import numpy as np
import jax
import jax.numpy as jnp
from jax import lax
from jax.experimental import pallas as pl
from jax.experimental.pallas import tpu as pltpu
from jax.sharding import PartitionSpec as P

ROUNDS = 8
CHUNKS = 2
NN = (((1,), (0,)), ((), ()))
NT = (((1,), (1,)), ((), ()))


def inverse_coefficients(degree):
    cheb = np.polynomial.chebyshev.Chebyshev.basis(degree + 1).convert(kind=np.polynomial.Polynomial)
    shifted = cheb(np.polynomial.Polynomial([-1.0, 8.0]))
    residual = shifted / shifted(-1.0)
    quotient = (np.polynomial.Polynomial([1.0]) - residual) // np.polynomial.Polynomial([1.0, 1.0])
    return [float(c) for c in quotient.coef]


def split(a):
    high = a.astype(jnp.bfloat16)
    return high, (a - high.astype(jnp.float32)).astype(jnp.bfloat16)


def dot3(a, b, dims):
    (ah, al), (bh, bl) = a, b
    dot = functools.partial(lax.dot_general, dimension_numbers=dims, preferred_element_type=jnp.float32)
    return dot(ah, bh) + (dot(ah, bl) + dot(al, bh))


def whole_kernel(n, nz, half, cw, fwd_ref, adj_ref, out_ref, topbuf, botbuf, outtop, outbot, stats,
                 fwd_t, gathered, part, parts_in,
                 send_r, recv_t, send_l, recv_b, send_z, recv_z, gsend, grecv, psend, precv):
    s = lax.axis_index("snap")
    z = lax.axis_index("zone")
    coef = inverse_coefficients(6)
    length = n // 4
    zc = s // 4
    y = (s // 2) % 2
    core = s % 2
    across = s + 2 - 4 * y
    sibling = s + 1 - 2 * core
    across_sibling = across + 1 - 2 * core
    per = n // nz
    bw = 2 * half

    barrier = pltpu.get_barrier_semaphore()

    @pl.when(s > 0)
    def _():
        pl.semaphore_signal(barrier, inc=1, device_id={"snap": s - 1}, device_id_type=pl.DeviceIdType.MESH)

    @pl.when(s < n - 1)
    def _():
        pl.semaphore_signal(barrier, inc=1, device_id={"snap": s + 1}, device_id_type=pl.DeviceIdType.MESH)

    @pl.when(zc > 0)
    def _():
        pl.semaphore_signal(barrier, inc=1, device_id={"snap": s - 4}, device_id_type=pl.DeviceIdType.MESH)

    @pl.when(zc < length - 1)
    def _():
        pl.semaphore_signal(barrier, inc=1, device_id={"snap": s + 4}, device_id_type=pl.DeviceIdType.MESH)

    pl.semaphore_signal(barrier, inc=1, device_id={"snap": across}, device_id_type=pl.DeviceIdType.MESH)
    pl.semaphore_signal(barrier, inc=1, device_id={"snap": sibling}, device_id_type=pl.DeviceIdType.MESH)
    for k in range(1, nz):
        pl.semaphore_signal(barrier, inc=1, device_id={"zone": lax.rem(z + k, nz)}, device_id_type=pl.DeviceIdType.MESH)
    greeted = (nz + 1 + jnp.minimum(s, 1) + jnp.minimum(n - 1 - s, 1)
               + jnp.minimum(zc, 1) + jnp.minimum(length - 1 - zc, 1))
    pl.semaphore_wait(barrier, greeted)

    pending = []

    def guarded(guard, action):
        if guard is None:
            action()
        else:
            pl.when(guard)(action)

    def both(a, b):
        return b if a is None else a & b

    def send_block(guard, src, kind, target):
        def copy():
            return pltpu.make_async_remote_copy(
                src_ref=adj_ref if src is s else gathered.at[src], dst_ref=gathered.at[src],
                send_sem=gsend.at[kind, src], recv_sem=grecv.at[src],
                device_id={"snap": target}, device_id_type=pl.DeviceIdType.MESH)
        guarded(guard, lambda: copy().start())
        pending.append((guard, copy))

    def await_block(guard, src):
        guarded(guard, lambda: pltpu.make_async_remote_copy(
            src_ref=gathered.at[src], dst_ref=gathered.at[src],
            send_sem=gsend.at[0, src], recv_sem=grecv.at[src],
            device_id={"snap": sibling}, device_id_type=pl.DeviceIdType.MESH).wait_recv())

    def part_copy(src):
        owner = src // per
        slot = (owner - z + nz) % nz
        return pltpu.make_async_remote_copy(
            src_ref=part.at[src], dst_ref=parts_in.at[slot, src % per],
            send_sem=psend.at[src], recv_sem=precv.at[slot, src % per],
            device_id={"zone": owner}, device_id_type=pl.DeviceIdType.MESH)

    def multiply(guard, src):
        def action():
            block = adj_ref[...] if src is s else gathered[src]
            part[src] = lax.dot_general(fwd_t[...], block, NN, preferred_element_type=jnp.float32)

            @pl.when(src // per != z)
            def _():
                part_copy(src).start()
        guarded(guard, action)

    def at_distance(base, t):
        if t == 0:
            return [(None, base, 0)]
        return [(zc >= t, base - 4 * t, 1), (zc < length - t, base + 4 * t, -1)]

    send_block(zc < length - 1, s, 0, jnp.minimum(s + 4, n - 1))
    send_block(zc > 0, s, 1, jnp.maximum(s - 4, 0))
    send_block(None, s, 2, across)
    send_block(None, s, 3, sibling)
    fwd_t[...] = fwd_ref[...].T
    multiply(None, s)
    for t in range(length + 1):
        if 0 < t < length:
            for guard, src, way in at_distance(s, t):
                await_block(guard, src)
                if way > 0:
                    send_block(both(guard, zc < length - 1), src, 0, jnp.minimum(s + 4, n - 1))
                else:
                    send_block(both(guard, zc > 0), src, 1, jnp.maximum(s - 4, 0))
                send_block(guard, src, 2, across)
                send_block(guard, src, 3, sibling)
            for guard, src, way in at_distance(s, t):
                multiply(guard, src)
        if t > 0:
            for guard, src, way in at_distance(across, t - 1):
                await_block(guard, src)
                send_block(guard, src, 3, sibling)
                multiply(guard, src)
        if t < length:
            for guard, src, way in at_distance(sibling, t):
                await_block(guard, src)
                multiply(guard, src)
        if t > 0:
            for guard, src, way in at_distance(across_sibling, t - 1):
                await_block(guard, src)
                multiply(guard, src)

    for j in range(per):
        rows = part[z * per + j]
        for k in range(1, nz):
            pltpu.make_async_remote_copy(
                src_ref=parts_in.at[k, j], dst_ref=parts_in.at[k, j],
                send_sem=psend.at[0], recv_sem=precv.at[k, j],
                device_id={"zone": lax.rem(z + 1, nz)}, device_id_type=pl.DeviceIdType.MESH).wait_recv()
            rows = rows + parts_in[k, j]
        c, at = divmod(j * bw, cw)
        topbuf[0, c, :, at:at + bw] = rows[0:half]
        botbuf[0, c, :, at:at + bw] = rows[half:bw]

    def right_copy(r, c, src):
        return pltpu.make_async_remote_copy(
            src_ref=src.at[r, c], dst_ref=topbuf.at[r + 1, c], send_sem=send_r.at[r, c], recv_sem=recv_t.at[r + 1, c],
            device_id={"snap": jnp.minimum(s + 1, n - 1)}, device_id_type=pl.DeviceIdType.MESH)

    def left_copy(r, c):
        return pltpu.make_async_remote_copy(
            src_ref=outbot.at[r, c], dst_ref=botbuf.at[r + 1, c], send_sem=send_l.at[r, c], recv_sem=recv_b.at[r + 1, c],
            device_id={"snap": jnp.maximum(s - 1, 0)}, device_id_type=pl.DeviceIdType.MESH)

    def zone_copy(r, k):
        return pltpu.make_async_remote_copy(
            src_ref=stats.at[r, 0], dst_ref=stats.at[r, k], send_sem=send_z.at[r, k], recv_sem=recv_z.at[r, k],
            device_id={"zone": lax.rem(z + k, nz)}, device_id_type=pl.DeviceIdType.MESH)

    def rotate(r):
        block = None
        ones = jnp.ones((8, cw), jnp.bfloat16)
        for c in range(CHUNKS):
            top = topbuf[r, c]
            bottom = botbuf[r, c]
            part = dot3(split(top), split(bottom), NT)
            tops = jnp.sum(top * top, axis=1, keepdims=True)
            bh, bl = split(bottom * bottom)
            bots = (lax.dot_general(ones, bh, NT, preferred_element_type=jnp.float32)
                    + lax.dot_general(ones, bl, NT, preferred_element_type=jnp.float32))
            block, tsum, bsum = (part, tops, bots) if block is None else (block + part, tsum + tops, bsum + bots)
        stats[r, 0, 0:half, 0:half] = block
        stats[r, 0, 0:half, half:2 * half] = jnp.broadcast_to(tsum, (half, half))
        stats[r, 0, half:half + 8, 0:half] = bsum
        stats[r, 0, half:half + 8, half:2 * half] = bsum
        for k in range(1, nz):
            zone_copy(r, k).start()
        total = stats[r, 0]
        for k in range(1, nz):
            zone_copy(r, k).wait_recv()
            total = total + stats[r, k]
        tinv = 1.0 / jnp.sqrt(total[0:half, half:2 * half] + 1e-06)
        binv = 1.0 / jnp.sqrt(total[half:half + 1, 0:half] + 1e-06)
        corr = total[0:half, 0:half] * (tinv * binv)
        spread = jnp.sqrt(jnp.sum(corr * corr, keepdims=True))
        x = corr * (0.5 / jnp.maximum(spread, 1.0))
        xs = split(x)
        xts = split(x.T)
        ident = (lax.broadcasted_iota(jnp.int32, (half, half), 0)
                 == lax.broadcasted_iota(jnp.int32, (half, half), 1)).astype(jnp.float32)
        n1 = dot3(xs, xs, NT)
        n1s = split(n1)
        n2 = dot3(n1s, n1s, NN)
        n3 = dot3(split(n2), n1s, NN)
        upper = coef[3] * ident + coef[4] * n1 + coef[5] * n2 + coef[6] * n3
        inverse = coef[0] * ident + coef[1] * n1 + coef[2] * n2 + dot3(split(n3), split(upper), NN)
        invs = split(inverse)
        return xs, xts, invs

    def apply(r, c, parts):
        xs, xts, invs = parts
        top = topbuf[r, c]
        bottom = botbuf[r, c]
        v = top - dot3(xs, split(bottom), NN)
        w = dot3(invs, split(v), NN)
        return 2.0 * w - top, bottom + 2.0 * dot3(xts, split(w), NN)

    def step(r, carry):
        @pl.when((r > 0) & (s > 0))
        def _():
            for c in range(CHUNKS):
                right_copy(r - 1, c, outtop).wait_recv()

        @pl.when((r > 0) & (s < n - 1))
        def _():
            for c in range(CHUNKS):
                left_copy(r - 1, c).wait_recv()

        parts = rotate(r)
        for c in range(CHUNKS):
            top, bottom = apply(r, c, parts)
            outtop[r, c] = top
            outbot[r, c] = bottom

            @pl.when((s > 0) & (s < n - 1))
            def _():
                right_copy(r, c, outtop).start()

            @pl.when(s == 0)
            def _():
                right_copy(r, c, outbot).start()
                topbuf[r + 1, c] = outtop[r, c]

            @pl.when(s > 0)
            def _():
                left_copy(r, c).start()

            @pl.when(s == n - 1)
            def _():
                botbuf[r + 1, c] = outtop[r, c]
        return carry

    lax.fori_loop(0, ROUNDS - 1, step, 0)
    last = ROUNDS - 1

    @pl.when(s > 0)
    def _():
        for c in range(CHUNKS):
            right_copy(last - 1, c, outtop).wait_recv()

    @pl.when(s < n - 1)
    def _():
        for c in range(CHUNKS):
            left_copy(last - 1, c).wait_recv()

    parts = rotate(last)
    for c in range(CHUNKS):
        top, bottom = apply(last, c, parts)
        out_ref[0:half, c * cw:(c + 1) * cw] = top
        out_ref[half:2 * half, c * cw:(c + 1) * cw] = bottom

    def drain(r, carry):
        @pl.when(s < n - 1)
        def _():
            for c in range(CHUNKS):
                right_copy(r, c, outtop).wait_send()

        @pl.when(s > 0)
        def _():
            for c in range(CHUNKS):
                left_copy(r, c).wait_send()
        return carry

    lax.fori_loop(0, last, drain, 0)

    def drain_zone(r, carry):
        for k in range(1, nz):
            zone_copy(r, k).wait_send()
        return carry

    lax.fori_loop(0, ROUNDS, drain_zone, 0)

    for guard, copy in pending:
        guarded(guard, lambda: copy().wait_send())

    def drain_parts(src, carry):
        @pl.when(src // per != z)
        def _():
            part_copy(src).wait_send()
        return carry

    lax.fori_loop(0, n, drain_parts, 0)


def solution(mesh):
    n, nz = mesh.shape["snap"], mesh.shape["zone"]

    def shards(forward, adjoint):
        zones, bw = forward.shape
        half = bw // 2
        width = bw * n // nz
        cw = width // CHUNKS
        return pl.pallas_call(
            functools.partial(whole_kernel, n, nz, half, cw),
            out_shape=jax.ShapeDtypeStruct((bw, width), jnp.float32),
            in_specs=[pl.BlockSpec(memory_space=pltpu.VMEM)] * 2,
            out_specs=pl.BlockSpec(memory_space=pltpu.VMEM),
            scratch_shapes=[
                pltpu.VMEM((ROUNDS, CHUNKS, half, cw), jnp.float32),
                pltpu.VMEM((ROUNDS, CHUNKS, half, cw), jnp.float32),
                pltpu.VMEM((ROUNDS - 1, CHUNKS, half, cw), jnp.float32),
                pltpu.VMEM((ROUNDS - 1, CHUNKS, half, cw), jnp.float32),
                pltpu.VMEM((ROUNDS, nz, half + 8, 2 * half), jnp.float32),
                pltpu.VMEM((bw, zones), jnp.bfloat16),
                pltpu.VMEM((n, zones, bw), jnp.bfloat16),
                pltpu.VMEM((n, bw, bw), jnp.float32),
                pltpu.VMEM((nz, n // nz, bw, bw), jnp.float32),
                pltpu.SemaphoreType.DMA((ROUNDS, CHUNKS)),
                pltpu.SemaphoreType.DMA((ROUNDS, CHUNKS)),
                pltpu.SemaphoreType.DMA((ROUNDS, CHUNKS)),
                pltpu.SemaphoreType.DMA((ROUNDS, CHUNKS)),
                pltpu.SemaphoreType.DMA((ROUNDS, nz)),
                pltpu.SemaphoreType.DMA((ROUNDS, nz)),
                pltpu.SemaphoreType.DMA((4, n)),
                pltpu.SemaphoreType.DMA((n,)),
                pltpu.SemaphoreType.DMA((n,)),
                pltpu.SemaphoreType.DMA((nz, n // nz)),
            ],
            compiler_params=pltpu.CompilerParams(
                collective_id=0, has_side_effects=True, vmem_limit_bytes=48 * 1024 * 1024),
        )(forward, adjoint)

    return jax.shard_map(
        shards,
        mesh=mesh,
        in_specs=(P("zone", "snap"), P("zone", "snap")),
        out_specs=P("snap", "zone"),
        check_vma=False,
    )
```

```python
import functools

import numpy as np
import jax
import jax.numpy as jnp
from jax import lax
from jax.experimental import pallas as pl
from jax.experimental.pallas import tpu as pltpu
from jax.sharding import PartitionSpec as P

ROUNDS = 8
CHUNKS = 2
NN = (((1,), (0,)), ((), ()))
NT = (((1,), (1,)), ((), ()))


def inverse_coefficients(degree):
    cheb = np.polynomial.chebyshev.Chebyshev.basis(degree + 1).convert(kind=np.polynomial.Polynomial)
    shifted = cheb(np.polynomial.Polynomial([-1.0, 8.0]))
    residual = shifted / shifted(-1.0)
    quotient = (np.polynomial.Polynomial([1.0]) - residual) // np.polynomial.Polynomial([1.0, 1.0])
    return [float(c) for c in quotient.coef]


def split(a):
    high = a.astype(jnp.bfloat16)
    return high, (a - high.astype(jnp.float32)).astype(jnp.bfloat16)


def dot3(a, b, dims):
    (ah, al), (bh, bl) = a, b
    dot = functools.partial(lax.dot_general, dimension_numbers=dims, preferred_element_type=jnp.float32)
    return dot(ah, bh) + (dot(ah, bl) + dot(al, bh))


def dot1(a, b):
    return lax.dot_general(a, b, NT, preferred_element_type=jnp.float32)


def whole_kernel(n, nz, half, cw, fwd_ref, adj_ref, out_ref, topbuf, botbuf, outtop, outbot, stats,
                 fwd_t, gathered, part, parts_in,
                 send_r, recv_t, send_l, recv_b, send_z, recv_z, gsend, grecv, psend, precv):
    s = lax.axis_index("snap")
    z = lax.axis_index("zone")
    coef = inverse_coefficients(6)
    length = n // 4
    zc = s // 4
    y = (s // 2) % 2
    core = s % 2
    across = s + 2 - 4 * y
    sibling = s + 1 - 2 * core
    across_sibling = across + 1 - 2 * core
    per = n // nz
    bw = 2 * half
    short = half // 2

    barrier = pltpu.get_barrier_semaphore()

    @pl.when(s > 0)
    def _():
        pl.semaphore_signal(barrier, inc=1, device_id={"snap": s - 1}, device_id_type=pl.DeviceIdType.MESH)

    @pl.when(s < n - 1)
    def _():
        pl.semaphore_signal(barrier, inc=1, device_id={"snap": s + 1}, device_id_type=pl.DeviceIdType.MESH)

    @pl.when(zc > 0)
    def _():
        pl.semaphore_signal(barrier, inc=1, device_id={"snap": s - 4}, device_id_type=pl.DeviceIdType.MESH)

    @pl.when(zc < length - 1)
    def _():
        pl.semaphore_signal(barrier, inc=1, device_id={"snap": s + 4}, device_id_type=pl.DeviceIdType.MESH)

    pl.semaphore_signal(barrier, inc=1, device_id={"snap": across}, device_id_type=pl.DeviceIdType.MESH)
    pl.semaphore_signal(barrier, inc=1, device_id={"snap": sibling}, device_id_type=pl.DeviceIdType.MESH)
    for k in range(1, nz):
        pl.semaphore_signal(barrier, inc=1, device_id={"zone": lax.rem(z + k, nz)}, device_id_type=pl.DeviceIdType.MESH)
    greeted = (nz + 1 + jnp.minimum(s, 1) + jnp.minimum(n - 1 - s, 1)
               + jnp.minimum(zc, 1) + jnp.minimum(length - 1 - zc, 1))
    pl.semaphore_wait(barrier, greeted)

    pending = []

    def guarded(guard, action):
        if guard is None:
            action()
        else:
            pl.when(guard)(action)

    def both(a, b):
        return b if a is None else a & b

    def send_block(guard, src, kind, target):
        def copy():
            return pltpu.make_async_remote_copy(
                src_ref=adj_ref if src is s else gathered.at[src], dst_ref=gathered.at[src],
                send_sem=gsend.at[kind, src], recv_sem=grecv.at[src],
                device_id={"snap": target}, device_id_type=pl.DeviceIdType.MESH)
        guarded(guard, lambda: copy().start())
        pending.append((guard, copy))

    def await_block(guard, src):
        guarded(guard, lambda: pltpu.make_async_remote_copy(
            src_ref=gathered.at[src], dst_ref=gathered.at[src],
            send_sem=gsend.at[0, src], recv_sem=grecv.at[src],
            device_id={"snap": sibling}, device_id_type=pl.DeviceIdType.MESH).wait_recv())

    def part_copy(src):
        owner = src // per
        slot = (owner - z + nz) % nz
        return pltpu.make_async_remote_copy(
            src_ref=part.at[src], dst_ref=parts_in.at[slot, src % per],
            send_sem=psend.at[src], recv_sem=precv.at[slot, src % per],
            device_id={"zone": owner}, device_id_type=pl.DeviceIdType.MESH)

    def multiply(guard, src):
        def action():
            block = adj_ref[...] if src is s else gathered[src]
            part[src] = lax.dot_general(fwd_t[...], block, NN, preferred_element_type=jnp.float32)

            @pl.when(src // per != z)
            def _():
                part_copy(src).start()
        guarded(guard, action)

    def at_distance(base, t):
        if t == 0:
            return [(None, base, 0)]
        return [(zc >= t, base - 4 * t, 1), (zc < length - t, base + 4 * t, -1)]

    send_block(zc < length - 1, s, 0, jnp.minimum(s + 4, n - 1))
    send_block(zc > 0, s, 1, jnp.maximum(s - 4, 0))
    send_block(None, s, 2, across)
    send_block(None, s, 3, sibling)
    fwd_t[...] = fwd_ref[...].T
    multiply(None, s)
    for t in range(length + 1):
        if 0 < t < length:
            for guard, src, way in at_distance(s, t):
                await_block(guard, src)
                if way > 0:
                    send_block(both(guard, zc < length - 1), src, 0, jnp.minimum(s + 4, n - 1))
                else:
                    send_block(both(guard, zc > 0), src, 1, jnp.maximum(s - 4, 0))
                send_block(guard, src, 2, across)
                send_block(guard, src, 3, sibling)
            for guard, src, way in at_distance(s, t):
                multiply(guard, src)
        if t > 0:
            for guard, src, way in at_distance(across, t - 1):
                await_block(guard, src)
                send_block(guard, src, 3, sibling)
                multiply(guard, src)
        if t < length:
            for guard, src, way in at_distance(sibling, t):
                await_block(guard, src)
                multiply(guard, src)
        if t > 0:
            for guard, src, way in at_distance(across_sibling, t - 1):
                await_block(guard, src)
                multiply(guard, src)

    for j in range(per):
        rows = part[z * per + j]
        for k in range(1, nz):
            pltpu.make_async_remote_copy(
                src_ref=parts_in.at[k, j], dst_ref=parts_in.at[k, j],
                send_sem=psend.at[0], recv_sem=precv.at[k, j],
                device_id={"zone": lax.rem(z + 1, nz)}, device_id_type=pl.DeviceIdType.MESH).wait_recv()
            rows = rows + parts_in[k, j]
        c, at = divmod(j * bw, cw)
        topbuf[0, c, :, at:at + bw] = rows[0:half]
        botbuf[0, c, :, at:at + bw] = rows[half:bw]

    def right_copy(r, c, src):
        return pltpu.make_async_remote_copy(
            src_ref=src.at[r, c], dst_ref=topbuf.at[r + 1, c], send_sem=send_r.at[r, c], recv_sem=recv_t.at[r + 1, c],
            device_id={"snap": jnp.minimum(s + 1, n - 1)}, device_id_type=pl.DeviceIdType.MESH)

    def left_copy(r, c):
        return pltpu.make_async_remote_copy(
            src_ref=outbot.at[r, c], dst_ref=botbuf.at[r + 1, c], send_sem=send_l.at[r, c], recv_sem=recv_b.at[r + 1, c],
            device_id={"snap": jnp.maximum(s - 1, 0)}, device_id_type=pl.DeviceIdType.MESH)

    def zone_copy(r, k):
        return pltpu.make_async_remote_copy(
            src_ref=stats.at[r, 0], dst_ref=stats.at[r, k], send_sem=send_z.at[r, k], recv_sem=recv_z.at[r, k],
            device_id={"zone": lax.rem(z + k, nz)}, device_id_type=pl.DeviceIdType.MESH)

    def settle(r):
        @pl.when(r == 0)
        def _():
            for guard, copy in pending:
                guarded(guard, lambda: copy().wait_send())

            def parts_sent(src, carry):
                @pl.when(src // per != z)
                def _():
                    part_copy(src).wait_send()
                return carry

            lax.fori_loop(0, n, parts_sent, 0)

        @pl.when((r > 0) & (s < n - 1))
        def _():
            for c in range(CHUNKS):
                right_copy(r - 1, c, outtop).wait_send()

        @pl.when((r > 0) & (s > 0))
        def _():
            for c in range(CHUNKS):
                left_copy(r - 1, c).wait_send()

        @pl.when(r > 0)
        def _():
            for k in range(1, nz):
                zone_copy(r - 1, k).wait_send()

    def take(r, c):
        @pl.when((r > 0) & (s > 0))
        def _():
            right_copy(r - 1, c, outtop).wait_recv()

        @pl.when((r > 0) & (s < n - 1))
        def _():
            left_copy(r - 1, c).wait_recv()

    def rotate(r):
        block = None
        ones = jnp.ones((8, cw), jnp.bfloat16)
        for c in range(CHUNKS):
            take(r, c)
            top = topbuf[r, c]
            bottom = botbuf[r, c]
            part = dot3(split(top), split(bottom), NT)
            th, tl = split(top * top)
            tops = dot1(ones, th) + dot1(ones, tl)
            bh, bl = split(bottom * bottom)
            bots = dot1(ones, bh) + dot1(ones, bl)
            block, tsum, bsum = (part, tops, bots) if block is None else (block + part, tsum + tops, bsum + bots)
        stats[r, 0, 0:short, 0:half] = block[0:short]
        stats[r, 0, 0:short, half:2 * half] = block[short:half]
        stats[r, 0, short:short + 8, 0:half] = tsum
        stats[r, 0, short:short + 8, half:2 * half] = bsum
        for k in range(1, nz):
            zone_copy(r, k).start()
        settle(r)
        total = stats[r, 0]
        for k in range(1, nz):
            zone_copy(r, k).wait_recv()
            total = total + stats[r, k]
        inv = 1.0 / jnp.sqrt(total[short:short + 1] + 1e-06)
        tinv = jnp.broadcast_to(inv[:, 0:half], (half, half)).T
        gram = jnp.concatenate([total[0:short, 0:half], total[0:short, half:2 * half]], axis=0)
        corr = gram * (tinv * inv[:, half:2 * half])
        spread = jnp.sqrt(jnp.sum(corr * corr, keepdims=True))
        x = corr * (0.5 / jnp.maximum(spread, 1.0))
        xs = split(x)
        xts = split(x.T)
        ident = (lax.broadcasted_iota(jnp.int32, (half, half), 0)
                 == lax.broadcasted_iota(jnp.int32, (half, half), 1)).astype(jnp.float32)
        n1 = dot3(xs, xs, NT)
        n1s = split(n1)
        n2 = dot3(n1s, n1s, NN)
        mixed = [topbuf[r, c] - dot3(xs, split(botbuf[r, c]), NN) for c in range(CHUNKS)]
        n3 = dot3(split(n2), n1s, NN)
        upper = coef[3] * ident + coef[4] * n1 + coef[5] * n2 + coef[6] * n3
        inverse = coef[0] * ident + coef[1] * n1 + coef[2] * n2 + dot3(split(n3), split(upper), NN)
        invs = split(inverse)
        return xts, invs, mixed

    def apply(r, c, parts):
        xts, invs, mixed = parts
        top = topbuf[r, c]
        bottom = botbuf[r, c]
        w = dot3(invs, split(mixed[c]), NN)
        return 2.0 * w - top, bottom + 2.0 * dot3(xts, split(w), NN)

    def step(r, carry):
        parts = rotate(r)
        for c in range(CHUNKS):
            top, bottom = apply(r, c, parts)
            outtop[r, c] = top
            outbot[r, c] = bottom

            @pl.when((s > 0) & (s < n - 1))
            def _():
                right_copy(r, c, outtop).start()

            @pl.when(s == 0)
            def _():
                right_copy(r, c, outbot).start()
                topbuf[r + 1, c] = outtop[r, c]

            @pl.when(s > 0)
            def _():
                left_copy(r, c).start()

            @pl.when(s == n - 1)
            def _():
                botbuf[r + 1, c] = outtop[r, c]
        return carry

    lax.fori_loop(0, ROUNDS - 1, step, 0)
    last = ROUNDS - 1

    parts = rotate(last)
    for c in range(CHUNKS):
        top, bottom = apply(last, c, parts)
        out_ref[0:half, c * cw:(c + 1) * cw] = top
        out_ref[half:2 * half, c * cw:(c + 1) * cw] = bottom

    for k in range(1, nz):
        zone_copy(last, k).wait_send()


def solution(mesh):
    n, nz = mesh.shape["snap"], mesh.shape["zone"]

    def shards(forward, adjoint):
        zones, bw = forward.shape
        half = bw // 2
        width = bw * n // nz
        cw = width // CHUNKS
        return pl.pallas_call(
            functools.partial(whole_kernel, n, nz, half, cw),
            out_shape=jax.ShapeDtypeStruct((bw, width), jnp.float32),
            in_specs=[pl.BlockSpec(memory_space=pltpu.VMEM)] * 2,
            out_specs=pl.BlockSpec(memory_space=pltpu.VMEM),
            scratch_shapes=[
                pltpu.VMEM((ROUNDS, CHUNKS, half, cw), jnp.float32),
                pltpu.VMEM((ROUNDS, CHUNKS, half, cw), jnp.float32),
                pltpu.VMEM((ROUNDS - 1, CHUNKS, half, cw), jnp.float32),
                pltpu.VMEM((ROUNDS - 1, CHUNKS, half, cw), jnp.float32),
                pltpu.VMEM((ROUNDS, nz, half // 2 + 8, 2 * half), jnp.float32),
                pltpu.VMEM((bw, zones), jnp.bfloat16),
                pltpu.VMEM((n, zones, bw), jnp.bfloat16),
                pltpu.VMEM((n, bw, bw), jnp.float32),
                pltpu.VMEM((nz, n // nz, bw, bw), jnp.float32),
                pltpu.SemaphoreType.DMA((ROUNDS, CHUNKS)),
                pltpu.SemaphoreType.DMA((ROUNDS, CHUNKS)),
                pltpu.SemaphoreType.DMA((ROUNDS, CHUNKS)),
                pltpu.SemaphoreType.DMA((ROUNDS, CHUNKS)),
                pltpu.SemaphoreType.DMA((ROUNDS, nz)),
                pltpu.SemaphoreType.DMA((ROUNDS, nz)),
                pltpu.SemaphoreType.DMA((4, n)),
                pltpu.SemaphoreType.DMA((n,)),
                pltpu.SemaphoreType.DMA((n,)),
                pltpu.SemaphoreType.DMA((nz, n // nz)),
            ],
            compiler_params=pltpu.CompilerParams(
                collective_id=0, has_side_effects=True, vmem_limit_bytes=48 * 1024 * 1024),
        )(forward, adjoint)

    return jax.shard_map(
        shards,
        mesh=mesh,
        in_specs=(P("zone", "snap"), P("zone", "snap")),
        out_specs=P("snap", "zone"),
        check_vma=False,
    )
```

```python
import functools

import numpy as np
import jax
import jax.numpy as jnp
from jax import lax
from jax.experimental import pallas as pl
from jax.experimental.pallas import tpu as pltpu
from jax.sharding import PartitionSpec as P

ROUNDS = 8
CHUNKS = 4
NN = (((1,), (0,)), ((), ()))
NT = (((1,), (1,)), ((), ()))


def inverse_coefficients(degree):
    cheb = np.polynomial.chebyshev.Chebyshev.basis(degree + 1).convert(kind=np.polynomial.Polynomial)
    shifted = cheb(np.polynomial.Polynomial([-1.0, 8.0]))
    residual = shifted / shifted(-1.0)
    quotient = (np.polynomial.Polynomial([1.0]) - residual) // np.polynomial.Polynomial([1.0, 1.0])
    return [float(c) for c in quotient.coef]


def split(a):
    high = a.astype(jnp.bfloat16)
    return high, (a - high.astype(jnp.float32)).astype(jnp.bfloat16)


def dot3(a, b, dims):
    (ah, al), (bh, bl) = a, b
    dot = functools.partial(lax.dot_general, dimension_numbers=dims, preferred_element_type=jnp.float32)
    return dot(ah, bh) + (dot(ah, bl) + dot(al, bh))


def dot1(a, b):
    return lax.dot_general(a, b, NT, preferred_element_type=jnp.float32)


def whole_kernel(n, nz, half, cw, fwd_ref, adj_ref, out_ref, topbuf, botbuf, outtop, outbot, stats,
                 fwd_t, gathered, part, parts_in,
                 send_r, recv_t, send_l, recv_b, send_z, recv_z, gsend, grecv, psend, precv):
    s = lax.axis_index("snap")
    z = lax.axis_index("zone")
    coef = inverse_coefficients(6)
    length = n // 4
    zc = s // 4
    y = (s // 2) % 2
    core = s % 2
    across = s + 2 - 4 * y
    sibling = s + 1 - 2 * core
    across_sibling = across + 1 - 2 * core
    per = n // nz
    bw = 2 * half
    short = half // 2

    barrier = pltpu.get_barrier_semaphore()

    @pl.when(s > 0)
    def _():
        pl.semaphore_signal(barrier, inc=1, device_id={"snap": s - 1}, device_id_type=pl.DeviceIdType.MESH)

    @pl.when(s < n - 1)
    def _():
        pl.semaphore_signal(barrier, inc=1, device_id={"snap": s + 1}, device_id_type=pl.DeviceIdType.MESH)

    @pl.when(zc > 0)
    def _():
        pl.semaphore_signal(barrier, inc=1, device_id={"snap": s - 4}, device_id_type=pl.DeviceIdType.MESH)

    @pl.when(zc < length - 1)
    def _():
        pl.semaphore_signal(barrier, inc=1, device_id={"snap": s + 4}, device_id_type=pl.DeviceIdType.MESH)

    pl.semaphore_signal(barrier, inc=1, device_id={"snap": across}, device_id_type=pl.DeviceIdType.MESH)
    pl.semaphore_signal(barrier, inc=1, device_id={"snap": sibling}, device_id_type=pl.DeviceIdType.MESH)
    for k in range(1, nz):
        pl.semaphore_signal(barrier, inc=1, device_id={"zone": lax.rem(z + k, nz)}, device_id_type=pl.DeviceIdType.MESH)
    greeted = (nz + 1 + jnp.minimum(s, 1) + jnp.minimum(n - 1 - s, 1)
               + jnp.minimum(zc, 1) + jnp.minimum(length - 1 - zc, 1))
    pl.semaphore_wait(barrier, greeted)

    pending = []

    def guarded(guard, action):
        if guard is None:
            action()
        else:
            pl.when(guard)(action)

    def both(a, b):
        return b if a is None else a & b

    def send_block(guard, src, kind, target):
        def copy():
            return pltpu.make_async_remote_copy(
                src_ref=adj_ref if src is s else gathered.at[src], dst_ref=gathered.at[src],
                send_sem=gsend.at[kind, src], recv_sem=grecv.at[src],
                device_id={"snap": target}, device_id_type=pl.DeviceIdType.MESH)
        guarded(guard, lambda: copy().start())
        pending.append((guard, copy))

    def await_block(guard, src):
        guarded(guard, lambda: pltpu.make_async_remote_copy(
            src_ref=gathered.at[src], dst_ref=gathered.at[src],
            send_sem=gsend.at[0, src], recv_sem=grecv.at[src],
            device_id={"snap": sibling}, device_id_type=pl.DeviceIdType.MESH).wait_recv())

    def part_copy(src):
        owner = src // per
        slot = (owner - z + nz) % nz
        return pltpu.make_async_remote_copy(
            src_ref=part.at[src], dst_ref=parts_in.at[slot, src % per],
            send_sem=psend.at[src], recv_sem=precv.at[slot, src % per],
            device_id={"zone": owner}, device_id_type=pl.DeviceIdType.MESH)

    def multiply(guard, src):
        def action():
            block = adj_ref[...] if src is s else gathered[src]
            part[src] = lax.dot_general(fwd_t[...], block, NN, preferred_element_type=jnp.float32)

            @pl.when(src // per != z)
            def _():
                part_copy(src).start()
        guarded(guard, action)

    def at_distance(base, t):
        if t == 0:
            return [(None, base, 0)]
        return [(zc >= t, base - 4 * t, 1), (zc < length - t, base + 4 * t, -1)]

    send_block(zc < length - 1, s, 0, jnp.minimum(s + 4, n - 1))
    send_block(zc > 0, s, 1, jnp.maximum(s - 4, 0))
    send_block(None, s, 2, across)
    send_block(None, s, 3, sibling)
    fwd_t[...] = fwd_ref[...].T
    multiply(None, s)
    for t in range(length + 1):
        if 0 < t < length:
            for guard, src, way in at_distance(s, t):
                await_block(guard, src)
                if way > 0:
                    send_block(both(guard, zc < length - 1), src, 0, jnp.minimum(s + 4, n - 1))
                else:
                    send_block(both(guard, zc > 0), src, 1, jnp.maximum(s - 4, 0))
                send_block(guard, src, 2, across)
                send_block(guard, src, 3, sibling)
            for guard, src, way in at_distance(s, t):
                multiply(guard, src)
        if t > 0:
            for guard, src, way in at_distance(across, t - 1):
                await_block(guard, src)
                send_block(guard, src, 3, sibling)
                multiply(guard, src)
        if t < length:
            for guard, src, way in at_distance(sibling, t):
                await_block(guard, src)
                multiply(guard, src)
        if t > 0:
            for guard, src, way in at_distance(across_sibling, t - 1):
                await_block(guard, src)
                multiply(guard, src)

    for j in range(per):
        rows = part[z * per + j]
        for k in range(1, nz):
            pltpu.make_async_remote_copy(
                src_ref=parts_in.at[k, j], dst_ref=parts_in.at[k, j],
                send_sem=psend.at[0], recv_sem=precv.at[k, j],
                device_id={"zone": lax.rem(z + 1, nz)}, device_id_type=pl.DeviceIdType.MESH).wait_recv()
            rows = rows + parts_in[k, j]
        c, at = divmod(j * bw, cw)
        topbuf[0, c, :, at:at + bw] = rows[0:half]
        botbuf[0, c, :, at:at + bw] = rows[half:bw]

    def right_copy(r, c, src):
        return pltpu.make_async_remote_copy(
            src_ref=src.at[r, c], dst_ref=topbuf.at[r + 1, c], send_sem=send_r.at[r, c], recv_sem=recv_t.at[r + 1, c],
            device_id={"snap": jnp.minimum(s + 1, n - 1)}, device_id_type=pl.DeviceIdType.MESH)

    def left_copy(r, c):
        return pltpu.make_async_remote_copy(
            src_ref=outbot.at[r, c], dst_ref=botbuf.at[r + 1, c], send_sem=send_l.at[r, c], recv_sem=recv_b.at[r + 1, c],
            device_id={"snap": jnp.maximum(s - 1, 0)}, device_id_type=pl.DeviceIdType.MESH)

    def zone_copy(r, k):
        return pltpu.make_async_remote_copy(
            src_ref=stats.at[r, 0], dst_ref=stats.at[r, k], send_sem=send_z.at[r, k], recv_sem=recv_z.at[r, k],
            device_id={"zone": lax.rem(z + k, nz)}, device_id_type=pl.DeviceIdType.MESH)

    def settle(r):
        @pl.when(r == 0)
        def _():
            for guard, copy in pending:
                guarded(guard, lambda: copy().wait_send())

            def parts_sent(src, carry):
                @pl.when(src // per != z)
                def _():
                    part_copy(src).wait_send()
                return carry

            lax.fori_loop(0, n, parts_sent, 0)

        @pl.when((r > 0) & (s < n - 1))
        def _():
            for c in range(CHUNKS):
                right_copy(r - 1, c, outtop).wait_send()

        @pl.when((r > 0) & (s > 0))
        def _():
            for c in range(CHUNKS):
                left_copy(r - 1, c).wait_send()

        @pl.when(r > 0)
        def _():
            for k in range(1, nz):
                zone_copy(r - 1, k).wait_send()

    def take(r, c):
        @pl.when((r > 0) & (s > 0))
        def _():
            right_copy(r - 1, c, outtop).wait_recv()

        @pl.when((r > 0) & (s < n - 1))
        def _():
            left_copy(r - 1, c).wait_recv()

    def rotate(r):
        block = None
        ones = jnp.ones((8, cw), jnp.bfloat16)
        for c in range(CHUNKS):
            take(r, c)
            top = topbuf[r, c]
            bottom = botbuf[r, c]
            part = dot3(split(top), split(bottom), NT)
            th, tl = split(top * top)
            tops = dot1(ones, th) + dot1(ones, tl)
            bh, bl = split(bottom * bottom)
            bots = dot1(ones, bh) + dot1(ones, bl)
            block, tsum, bsum = (part, tops, bots) if block is None else (block + part, tsum + tops, bsum + bots)
        stats[r, 0, 0:short, 0:half] = block[0:short]
        stats[r, 0, 0:short, half:2 * half] = block[short:half]
        stats[r, 0, short:short + 8, 0:half] = tsum
        stats[r, 0, short:short + 8, half:2 * half] = bsum
        for k in range(1, nz):
            zone_copy(r, k).start()
        settle(r)
        total = stats[r, 0]
        for k in range(1, nz):
            zone_copy(r, k).wait_recv()
            total = total + stats[r, k]
        inv = 1.0 / jnp.sqrt(total[short:short + 1] + 1e-06)
        tinv = jnp.broadcast_to(inv[:, 0:half], (half, half)).T
        gram = jnp.concatenate([total[0:short, 0:half], total[0:short, half:2 * half]], axis=0)
        corr = gram * (tinv * inv[:, half:2 * half])
        spread = jnp.sqrt(jnp.sum(corr * corr, keepdims=True))
        x = corr * (0.5 / jnp.maximum(spread, 1.0))
        xs = split(x)
        xts = split(x.T)
        ident = (lax.broadcasted_iota(jnp.int32, (half, half), 0)
                 == lax.broadcasted_iota(jnp.int32, (half, half), 1)).astype(jnp.float32)
        n1 = dot3(xs, xs, NT)
        n1s = split(n1)
        n2 = dot3(n1s, n1s, NN)
        mixed = [topbuf[r, c] - dot3(xs, split(botbuf[r, c]), NN) for c in range(CHUNKS)]
        n3 = dot3(split(n2), n1s, NN)
        upper = coef[3] * ident + coef[4] * n1 + coef[5] * n2 + coef[6] * n3
        inverse = coef[0] * ident + coef[1] * n1 + coef[2] * n2 + dot3(split(n3), split(upper), NN)
        invs = split(inverse)
        return xts, invs, mixed

    def apply(r, c, parts):
        xts, invs, mixed = parts
        top = topbuf[r, c]
        bottom = botbuf[r, c]
        w = dot3(invs, split(mixed[c]), NN)
        return 2.0 * w - top, bottom + 2.0 * dot3(xts, split(w), NN)

    def step(r, carry):
        parts = rotate(r)
        for c in range(CHUNKS):
            top, bottom = apply(r, c, parts)
            outtop[r, c] = top
            outbot[r, c] = bottom

            @pl.when((s > 0) & (s < n - 1))
            def _():
                right_copy(r, c, outtop).start()

            @pl.when(s == 0)
            def _():
                right_copy(r, c, outbot).start()
                topbuf[r + 1, c] = outtop[r, c]

            @pl.when(s > 0)
            def _():
                left_copy(r, c).start()

            @pl.when(s == n - 1)
            def _():
                botbuf[r + 1, c] = outtop[r, c]
        return carry

    lax.fori_loop(0, ROUNDS - 1, step, 0)
    last = ROUNDS - 1

    parts = rotate(last)
    for c in range(CHUNKS):
        top, bottom = apply(last, c, parts)
        out_ref[0:half, c * cw:(c + 1) * cw] = top
        out_ref[half:2 * half, c * cw:(c + 1) * cw] = bottom

    for k in range(1, nz):
        zone_copy(last, k).wait_send()


def solution(mesh):
    n, nz = mesh.shape["snap"], mesh.shape["zone"]

    def shards(forward, adjoint):
        zones, bw = forward.shape
        half = bw // 2
        width = bw * n // nz
        cw = width // CHUNKS
        return pl.pallas_call(
            functools.partial(whole_kernel, n, nz, half, cw),
            out_shape=jax.ShapeDtypeStruct((bw, width), jnp.float32),
            in_specs=[pl.BlockSpec(memory_space=pltpu.VMEM)] * 2,
            out_specs=pl.BlockSpec(memory_space=pltpu.VMEM),
            scratch_shapes=[
                pltpu.VMEM((ROUNDS, CHUNKS, half, cw), jnp.float32),
                pltpu.VMEM((ROUNDS, CHUNKS, half, cw), jnp.float32),
                pltpu.VMEM((ROUNDS - 1, CHUNKS, half, cw), jnp.float32),
                pltpu.VMEM((ROUNDS - 1, CHUNKS, half, cw), jnp.float32),
                pltpu.VMEM((ROUNDS, nz, half // 2 + 8, 2 * half), jnp.float32),
                pltpu.VMEM((bw, zones), jnp.bfloat16),
                pltpu.VMEM((n, zones, bw), jnp.bfloat16),
                pltpu.VMEM((n, bw, bw), jnp.float32),
                pltpu.VMEM((nz, n // nz, bw, bw), jnp.float32),
                pltpu.SemaphoreType.DMA((ROUNDS, CHUNKS)),
                pltpu.SemaphoreType.DMA((ROUNDS, CHUNKS)),
                pltpu.SemaphoreType.DMA((ROUNDS, CHUNKS)),
                pltpu.SemaphoreType.DMA((ROUNDS, CHUNKS)),
                pltpu.SemaphoreType.DMA((ROUNDS, nz)),
                pltpu.SemaphoreType.DMA((ROUNDS, nz)),
                pltpu.SemaphoreType.DMA((4, n)),
                pltpu.SemaphoreType.DMA((n,)),
                pltpu.SemaphoreType.DMA((n,)),
                pltpu.SemaphoreType.DMA((nz, n // nz)),
            ],
            compiler_params=pltpu.CompilerParams(
                collective_id=0, has_side_effects=True, vmem_limit_bytes=48 * 1024 * 1024),
        )(forward, adjoint)

    return jax.shard_map(
        shards,
        mesh=mesh,
        in_specs=(P("zone", "snap"), P("zone", "snap")),
        out_specs=P("snap", "zone"),
        check_vma=False,
    )
```
